32 devices in a mesh: dp: 4 (over y, x), ctx: 8 (over z, core).
Axes of the slice: x: 2, y: 2, z: 4, core: 2. Of those that a mesh axis runs over, the one named last changes fastest.
Arguments:
- queries: bfloat16 [8192, 128], P(('dp', 'ctx')), parts along dimension 0, may hold values from -6 to 6
- key_rows: bfloat16 [8192, 128], P(('dp', 'ctx')), parts along dimension 0, may hold values from -6 to 6
- value_rows: bfloat16 [8192, 128], P(('dp', 'ctx')), parts along dimension 0, may hold values from -0.5 to 0.5
- out_grad: bfloat16 [8192, 128], P(('dp', 'ctx')), parts along dimension 0, may hold values from -6 to 6
Outputs:
- query_grad: float32 [8192, 128], P(('dp', 'ctx')), parts along dimension 0
- key_grad: float32 [8192, 128], P(('dp', 'ctx')), parts along dimension 0
- value_grad: float32 [8192, 128], P(('dp', 'ctx')), parts along dimension 0
The draws below stay inside these ranges and needn't reach their ends.
There are 4 independent parts, one for each index of `dp`. The reference program is written for one: setup_inputs(seed, part) draws one part's arguments, and reference() takes and returns one part's arrays. A program takes and returns all parts, laid end to end along the dimension named above; each array names one. Nothing has to cross between parts.
All inputs are finite; a program needn't handle non-finite values.
Results may differ from the reference program's by a relative error of at most 0.0069.
Values may be sent and summed in bfloat16 or wider, within the bound.
No kernel may reach another device: no remote copies, remote signals or barrier semaphores. Data moves between devices by JAX's collectives and lax.ppermute only.
A program may use at most 64 MiB of HBM per device.

```python
import jax
import jax.numpy as jnp
from jax import lax

DH = 128
TOK_DEV = 256
SEQ = 2048


def drawn_pair(key):
    query_key = jax.random.fold_in(key, 101)
    other_key = jax.random.fold_in(key, 202)
    query_draw = jnp.clip(1.6 * jax.random.normal(query_key, (SEQ, DH), jnp.float32), -6.0, 6.0)
    key_draw = jnp.clip(1.6 * jax.random.normal(other_key, (SEQ, DH), jnp.float32), -6.0, 6.0)
    return (query_draw, key_draw)


def draw_queries(key, part):
    return drawn_pair(key)[0].astype(jnp.bfloat16)


def draw_key_rows(key, part):
    return drawn_pair(key)[1].astype(jnp.bfloat16)


def shard_levels(own_key, shape, shards, low, largest):
    loudness = 1.0
    for position, blocks in shards:
        heights = jax.random.uniform(jax.random.fold_in(jax.random.fold_in(own_key, 6), position), (blocks,), jnp.float32, low / len(shards), largest / len(shards))
        loudness = loudness * jnp.repeat(jnp.exp(heights), shape[position] // blocks).reshape((-1,) + (1,) * (len(shape) - 1 - position))
    return loudness


def scatter_about(stream_key, extent, deviation, most, pieces=(), held_as=jnp.bfloat16):
    drawn = deviation * jax.random.normal(stream_key, extent, jnp.float32)
    if pieces:
        drawn = drawn * shard_levels(stream_key, extent, pieces, -0.22, 0.18)
    return jnp.clip(drawn, -most, most).astype(held_as)


def setup_inputs(seed: int = 0, part: int = 0) -> dict:
    key_of = jax.random.split(jax.random.key(seed), 5)
    part_splits = jax.random.split(jax.random.fold_in(key_of[4], part), 5)
    queries = draw_queries(jax.random.fold_in(jax.random.fold_in(key_of[4], part), 71), part)
    key_rows = draw_key_rows(jax.random.fold_in(jax.random.fold_in(key_of[4], part), 71), part)
    value_rows = scatter_about(part_splits[2], (SEQ, DH), DH ** -0.5, 0.5, ((0, 8),))
    out_grad = scatter_about(part_splits[3], (SEQ, DH), 1.0, 6.0, ((0, 8),))
    return {"queries": queries, "key_rows": key_rows, "value_rows": value_rows, "out_grad": out_grad}


def reference(queries, key_rows, value_rows, out_grad):
    score_scale = DH ** -0.5
    blocks = SEQ // TOK_DEV
    query_blocks = queries.reshape(blocks, TOK_DEV, DH)
    grad_blocks = out_grad.reshape(blocks, TOK_DEV, DH)

    def one_block(carried, inputs):
        key_grad, value_grad = carried
        query_part, grad_part = inputs
        scores = jnp.dot(query_part, key_rows.T, preferred_element_type=jnp.float32) * score_scale
        prob_grad = jnp.dot(grad_part, value_rows.T, preferred_element_type=jnp.float32)
        row_peak = jnp.max(scores, axis=1)
        weights_now = jnp.exp(scores - row_peak[:, None])
        row_total = jnp.sum(weights_now, axis=1)
        log_total = row_peak + jnp.log(row_total)
        delta = jnp.sum(weights_now * prob_grad, axis=1) / row_total
        probs = jnp.exp(scores - log_total[:, None])
        score_grad = (probs * (prob_grad - delta[:, None])).astype(jnp.bfloat16)
        prob_half = probs.astype(jnp.bfloat16)
        query_grad = jnp.dot(score_grad, key_rows, preferred_element_type=jnp.float32) * score_scale
        key_grad = key_grad + jnp.dot(score_grad.T, query_part, preferred_element_type=jnp.float32)
        value_grad = value_grad + jnp.dot(prob_half.T, grad_part, preferred_element_type=jnp.float32)
        return (key_grad, value_grad), query_grad

    zero_grads = jnp.zeros((SEQ, DH), jnp.float32)
    (key_grad, value_grad), query_grad = lax.scan(one_block, (zero_grads, zero_grads), (query_blocks, grad_blocks))
    return query_grad.reshape(SEQ, DH), key_grad * score_scale, value_grad
```

```python
import functools

import jax
import jax.numpy as jnp
from jax import lax
from jax.experimental import pallas as pl
from jax.experimental.pallas import tpu as pltpu
from jax.sharding import PartitionSpec as P

LOG2_E = 1.4426950408889634


def dot_nt(left, right):
    return lax.dot_general(left, right, (((1,), (1,)), ((), ())), preferred_element_type=jnp.float32)


def dot_nn(left, right):
    return lax.dot_general(left, right, (((1,), (0,)), ((), ())), preferred_element_type=jnp.float32)


def dot_tn(left, right):
    return lax.dot_general(left, right, (((0,), (0,)), ((), ())), preferred_element_type=jnp.float32)


def by_sublane(reduce, tile):
    rows, cols = tile.shape
    return reduce(tile.reshape(rows // 8, 8, cols), axis=0)


def block_kernel(n_pieces, own, adds, *refs):
    refs = list(refs)
    query_ref, grad_ref = refs[:2]
    keys = refs[2 : 2 + n_pieces]
    values = refs[2 + n_pieces : 2 + 2 * n_pieces]
    rest = refs[2 + 2 * n_pieces :]
    sums_in = rest[:2] if adds else None
    rest = rest[2:] if adds else rest
    mine_ref, other_ref = rest[:2]
    dq_ref = rest[2] if own else None
    tiles, grads = rest[-2:]
    rows, width = query_ref.shape
    scale = width ** (-0.5)
    queries, out_grad = query_ref[...], grad_ref[...]

    peak = None
    for i, key_ref in enumerate(keys):
        scores = dot_nt(key_ref[...], queries)
        tiles[i] = scores
        top = by_sublane(jnp.max, scores)
        peak = top if peak is None else jnp.maximum(peak, top)
    peak = jnp.max(peak, axis=0, keepdims=True)
    factor = scale * LOG2_E
    shift = peak * factor
    kept = n_pieces if own else 2
    total, weighted = None, None
    for i, value_ref in enumerate(values):
        prob_grad = dot_nt(value_ref[...], out_grad)
        weights = jnp.exp2(tiles[i] * factor - shift)
        if i < kept:
            tiles[i] = weights
            grads[i] = prob_grad
        a, b = by_sublane(jnp.sum, weights), by_sublane(jnp.sum, weights * prob_grad)
        total = a if total is None else total + a
        weighted = b if weighted is None else weighted + b
    inverse = 1.0 / jnp.sum(total, axis=0, keepdims=True)
    delta = jnp.sum(weighted, axis=0, keepdims=True) * inverse
    dq = None
    for i in range(kept):
        probs = tiles[i] * inverse
        score_grad = (probs * (grads[i] - delta)).astype(jnp.bfloat16)
        if i < 2:
            out_ref = (mine_ref, other_ref)[i]
            dk = dot_nn(score_grad, queries)
            dv = dot_nn(probs.astype(jnp.bfloat16), out_grad)
            if adds:
                dk, dv = dk + sums_in[i][:rows], dv + sums_in[i][rows:]
            out_ref[:rows] = dk
            out_ref[rows:] = dv
        if own:
            part = dot_tn(keys[i][...], score_grad)
            dq = part if dq is None else dq + part
    if own:
        dq_ref[...] = dq.T * scale


def block_call(query, grad, keys, values, sums, own):
    rows, width = query.shape
    n = len(keys)
    adds = sums is not None
    pair = jax.ShapeDtypeStruct((2 * rows, width), jnp.float32)
    outs = [pair, pair] + ([jax.ShapeDtypeStruct((rows, width), jnp.float32)] if own else [])
    kept = n if own else 2
    args = [query, grad, *keys, *values] + (list(sums) if adds else [])
    flops = 2 * rows * rows * width * (2 * n + 4 + (n if own else 0))
    return pl.pallas_call(
        functools.partial(block_kernel, n, own, adds),
        out_shape=outs,
        in_specs=[pl.BlockSpec(memory_space=pltpu.VMEM)] * len(args),
        out_specs=[pl.BlockSpec(memory_space=pltpu.VMEM)] * len(outs),
        scratch_shapes=[pltpu.VMEM((n, rows, rows), jnp.float32), pltpu.VMEM((kept, rows, rows), jnp.float32)],
        cost_estimate=pl.CostEstimate(flops=flops, bytes_accessed=rows * width * 8 * n, transcendentals=rows * rows * n),
    )(*args)


def shards(queries, key_rows, value_rows, out_grad):
    size = lax.axis_size("ctx")

    def swap(x, bit):
        return lax.ppermute(x, "ctx", [(i, i ^ bit) for i in range(size)])

    bits = [1 << b for b in range(size.bit_length() - 2, 0, -1)]

    def spread(x):
        pieces = [x]
        for bit in bits:
            pieces += [swap(p, bit) for p in pieces]
        return pieces

    keys, values = spread(key_rows), spread(value_rows)
    query_blocks, grad_blocks = spread(queries), spread(out_grad)
    all_keys = [x for p in keys for x in (p, swap(p, 1))]
    all_values = [x for p in values for x in (p, swap(p, 1))]
    sums, query_grad = None, None
    for i, (query, grad) in enumerate(zip(query_blocks, grad_blocks)):
        mine, other, *dq = block_call(query, grad, all_keys, all_values, sums, i == 0)
        sums = (mine, other)
        query_grad = dq[0] if i == 0 else query_grad
    rows, width = queries.shape
    total = sums[0] + swap(sums[1], 1)
    return query_grad, total[:rows] * width ** (-0.5), total[rows:]


def solution(mesh):
    spec = P(("dp", "ctx"), None)
    return jax.shard_map(shards, mesh=mesh, in_specs=(spec,) * 4, out_specs=(spec,) * 3, check_vma=False)
```

```python
import functools

import jax
import jax.numpy as jnp
from jax import lax
from jax.experimental import pallas as pl
from jax.experimental.pallas import tpu as pltpu
from jax.sharding import PartitionSpec as P

LOG2_E = 1.4426950408889634


def dot_nt(left, right):
    return lax.dot_general(left, right, (((1,), (1,)), ((), ())), preferred_element_type=jnp.float32)


def dot_nn(left, right):
    return lax.dot_general(left, right, (((1,), (0,)), ((), ())), preferred_element_type=jnp.float32)


def dot_tn(left, right):
    return lax.dot_general(left, right, (((0,), (0,)), ((), ())), preferred_element_type=jnp.float32)


def by_sublane(reduce, tile):
    rows, cols = tile.shape
    return reduce(tile.reshape(rows // 8, 8, cols), axis=0)


def block_kernel(n_pieces, own, adds, *refs):
    refs = list(refs)
    query_ref, grad_ref = refs[:2]
    keys = refs[2 : 2 + n_pieces]
    values = refs[2 + n_pieces : 2 + 2 * n_pieces]
    rest = refs[2 + 2 * n_pieces :]
    sums_in = rest[:2] if adds else None
    rest = rest[2:] if adds else rest
    mine_ref, other_ref = rest[:2]
    dq_ref = rest[2] if own else None
    tiles, grads = rest[-2:]
    rows, width = query_ref.shape
    scale = width ** (-0.5)
    queries, out_grad = query_ref[...], grad_ref[...]

    peak = None
    for i, key_ref in enumerate(keys):
        scores = dot_nt(key_ref[...], queries)
        tiles[i] = scores
        top = by_sublane(jnp.max, scores)
        peak = top if peak is None else jnp.maximum(peak, top)
    peak = jnp.max(peak, axis=0, keepdims=True)
    factor = scale * LOG2_E
    shift = peak * factor
    kept = n_pieces if own else 2
    total, weighted = None, None
    for i, value_ref in enumerate(values):
        prob_grad = dot_nt(value_ref[...], out_grad)
        weights = jnp.exp2(tiles[i] * factor - shift)
        if i < kept:
            tiles[i] = weights
            grads[i] = prob_grad
        a, b = by_sublane(jnp.sum, weights), by_sublane(jnp.sum, weights * prob_grad)
        total = a if total is None else total + a
        weighted = b if weighted is None else weighted + b
    inverse = 1.0 / jnp.sum(total, axis=0, keepdims=True)
    delta = jnp.sum(weighted, axis=0, keepdims=True) * inverse
    dq = None
    for i in range(kept):
        probs = tiles[i] * inverse
        score_grad = (probs * (grads[i] - delta)).astype(jnp.bfloat16)
        if i < 2:
            out_ref = (mine_ref, other_ref)[i]
            dk = dot_nn(score_grad, queries)
            dv = dot_nn(probs.astype(jnp.bfloat16), out_grad)
            if adds:
                dk, dv = dk + sums_in[i][:rows], dv + sums_in[i][rows:]
            out_ref[:rows] = dk
            out_ref[rows:] = dv
        if own:
            part = dot_tn(keys[i][...], score_grad)
            dq = part if dq is None else dq + part
    if own:
        dq_ref[...] = dq.T * scale


def block_call(query, grad, keys, values, sums, own):
    rows, width = query.shape
    n = len(keys)
    adds = sums is not None
    pair = jax.ShapeDtypeStruct((2 * rows, width), jnp.float32)
    outs = [pair, pair] + ([jax.ShapeDtypeStruct((rows, width), jnp.float32)] if own else [])
    kept = n if own else 2
    args = [query, grad, *keys, *values] + (list(sums) if adds else [])
    flops = 2 * rows * rows * width * (2 * n + 4 + (n if own else 0))
    return pl.pallas_call(
        functools.partial(block_kernel, n, own, adds),
        out_shape=outs,
        in_specs=[pl.BlockSpec(memory_space=pltpu.VMEM)] * len(args),
        out_specs=[pl.BlockSpec(memory_space=pltpu.VMEM)] * len(outs),
        scratch_shapes=[pltpu.VMEM((n, rows, rows), jnp.float32), pltpu.VMEM((kept, rows, rows), jnp.float32)],
        compiler_params=pltpu.CompilerParams(vmem_limit_bytes=(n + kept) * rows * rows * 4 + (8 << 20)),
        cost_estimate=pl.CostEstimate(flops=flops, bytes_accessed=rows * width * 8 * n, transcendentals=rows * rows * n),
    )(*args)


def shards(queries, key_rows, value_rows, out_grad):
    size = lax.axis_size("ctx")

    def swap(x, bit):
        return lax.ppermute(x, "ctx", [(i, i ^ bit) for i in range(size)])

    bits = [1 << b for b in range(size.bit_length() - 2, 0, -1)]

    def spread(x):
        pieces = [x]
        for bit in bits:
            pieces += [swap(p, bit) for p in pieces]
        return pieces

    keys, values = spread(key_rows), spread(value_rows)
    query_blocks, grad_blocks = spread(queries), spread(out_grad)
    all_keys = [x for p in keys for x in (p, swap(p, 1))]
    all_values = [x for p in values for x in (p, swap(p, 1))]
    sums, query_grad = None, None
    for i, (query, grad) in enumerate(zip(query_blocks, grad_blocks)):
        mine, other, *dq = block_call(query, grad, all_keys, all_values, sums, i == 0)
        sums = (mine, other)
        query_grad = dq[0] if i == 0 else query_grad
    rows, width = queries.shape
    total = sums[0] + swap(sums[1], 1)
    return query_grad, total[:rows] * width ** (-0.5), total[rows:]


def solution(mesh):
    spec = P(("dp", "ctx"), None)
    return jax.shard_map(shards, mesh=mesh, in_specs=(spec,) * 4, out_specs=(spec,) * 3, check_vma=False)
```
